32 devices in a mesh: row: 2 (over core), col: 16 (over z, y, x).
Axes of the slice: x: 2, y: 2, z: 4, core: 2. Of those that a mesh axis runs over, the one named last changes fastest.
Arguments:
- tiles: bfloat16 [2, 2, 96, 128, 128], P(None, 'row', 'col'), may hold values from -0.21875 to 0.21875
- block_rows: int32 [2, 2, 96], P(None, 'row', 'col'), may hold values from 0 to 31, as said below
- block_cols: int32 [2, 2, 96], P(None, 'row', 'col'), may hold values from 0 to 15
- live_counts: int32 [2, 2, 16], P(None, 'row', 'col'), may hold values from 1 to 6, as said below
- panels: bfloat16 [2, 2048, 4096], P(None, 'row', 'col'), may hold values from -6 to 6
Outputs:
- voltages: float32 [8192, 4096], P('row', 'col')
The draws below stay inside these ranges and needn't reach their ends.
Inputs may be any that keep to these rules, and one draw needn't show every extreme that they name: `block_rows`: within one step and one bus-row group, all slots name distinct (block row, block column) pairs, and among them are block (0, 0) and block (31, 15). `live_counts`: in every step some bus-row group has all its slots live.
All inputs are finite; a program needn't handle non-finite values.
Results may differ from the reference program's by a relative error of at most 0.0003.
Values may be sent and summed in bfloat16 or wider, within the bound.
No kernel may reach another device: no remote copies, remote signals or barrier semaphores. Data moves between devices by JAX's collectives and lax.ppermute only.
A program may use at most 192 MiB of HBM per device.

```python
import jax
import jax.numpy as jnp
from jax import lax

BS = 128
PB = 16
STEPS = 2
RB_DEV = 32
NZ_DEV = 6
PANEL = 2048
SLOTS = 96
SCEN = 4096
N_ROW = 2
N_COL = 16


def one_pattern(sub):
    first, second = jax.random.split(sub)
    total_blocks = RB_DEV * PB
    middle = 1 + jax.random.permutation(first, total_blocks - 2)[:SLOTS - 2]
    picks = jnp.concatenate([jnp.array([0, total_blocks - 1], jnp.int32), middle.astype(jnp.int32)])
    order = jax.random.permutation(second, SLOTS)
    return picks[order]


def pattern(key):
    base = jax.random.fold_in(key, 7)
    keys = jax.random.split(base, STEPS * N_ROW)
    picks = jax.vmap(one_pattern)(keys)
    return picks.reshape(STEPS, N_ROW, SLOTS).astype(jnp.int32)


def draw_block_rows(key, part):
    return (pattern(key) // PB).astype(jnp.int32)


def draw_block_cols(key, part):
    return (pattern(key) % PB).astype(jnp.int32)


def draw_live_counts(key, part):
    first, second = jax.random.split(jax.random.fold_in(key, 11))
    counts = jax.random.randint(first, (STEPS, N_ROW, N_COL), 1, NZ_DEV + 1)
    busiest = jax.random.randint(second, (STEPS,), 0, N_ROW)
    full = jnp.arange(N_ROW)[None, :, None] == busiest[:, None, None]
    return jnp.where(full, NZ_DEV, counts).astype(jnp.int32)


def level_of(rng, extent, cuts, low, high):
    gain = 1.0
    for axis_at, blocks in cuts:
        draws = jax.random.uniform(jax.random.fold_in(jax.random.fold_in(rng, 6), axis_at), (blocks,), jnp.float32, low / len(cuts), high / len(cuts))
        gain = gain * jnp.repeat(jnp.exp(draws), extent[axis_at] // blocks).reshape((-1,) + (1,) * (len(extent) - 1 - axis_at))
    return gain


def normal_values(own_key, extent, width, reach, pieces=(), dtype=jnp.bfloat16):
    level = level_of(own_key, extent, pieces, -0.22, 0.18) if pieces else 1.0
    result = jax.random.normal(own_key, extent, jnp.float32) * width * level
    return jnp.minimum(jnp.maximum(result, -reach), reach).astype(dtype)


def setup_inputs(seed: int = 0) -> dict:
    key_of = jax.random.split(jax.random.key(seed), 6)
    return {
        "tiles": normal_values(key_of[0], (STEPS, N_ROW, SLOTS, BS, BS), (BS * NZ_DEV * N_COL * STEPS // RB_DEV) ** -0.5, 0.21875, ((1, 2), (2, 16))),
        "block_rows": draw_block_rows(jax.random.fold_in(key_of[5], 71), 0),
        "block_cols": draw_block_cols(jax.random.fold_in(key_of[5], 71), 0),
        "live_counts": draw_live_counts(jax.random.fold_in(key_of[5], 71), 0),
        "panels": normal_values(key_of[4], (STEPS, PANEL, SCEN), 1.0, 6.0, ((1, 2), (2, 16))),
    }


def reference(tiles, block_rows, block_cols, live_counts, panels):
    slot_ids = jnp.arange(SLOTS)
    owner = slot_ids // NZ_DEV
    within = slot_ids % NZ_DEV
    results = []
    for group in range(N_ROW):
        total = jnp.zeros((RB_DEV, BS, SCEN), jnp.float32)
        for step in range(STEPS):
            live = within < live_counts[step, group][owner]
            views = panels[step].reshape(PB, BS, SCEN)

            def add_slot(index, total, step=step, group=group, live=live, views=views):
                tile = tiles[step, group, index]
                picked = views[block_cols[step, group, index]]
                product = jnp.dot(tile, picked, preferred_element_type=jnp.float32)
                product = jnp.where(live[index], product, jnp.zeros_like(product))
                return total.at[block_rows[step, group, index]].add(product)

            total = lax.fori_loop(0, SLOTS, add_slot, total)
        results.append(total.reshape(RB_DEV * BS, SCEN))
    return jnp.concatenate(results, 0)
```

```python
import functools

import jax
import jax.numpy as jnp
from jax import lax
from jax.experimental import pallas as pl
from jax.experimental.pallas import tpu as pltpu
from jax.sharding import PartitionSpec as P

RB_DEV = 32
META = 16


def col_dims(n_col):
    return (4, 2, n_col // 8) if n_col % 8 == 0 else (n_col,)


def flat(dims, offset):
    index = 0
    for size, part in zip(dims, offset):
        index = index * size + part % size
    return index


def unflat(dims, index):
    parts = []
    for size in reversed(dims):
        parts.append(index % size)
        index //= size
    return tuple(reversed(parts))


def hop(dims, axis, unit):
    n_col = 1
    for size in dims:
        n_col *= size
    pairs = []
    for index in range(n_col):
        at = list(unflat(dims, index))
        at[axis] += 1
        pairs.append((index, flat(dims, at)))
    return lax.ppermute(unit, "col", pairs)


def back(dims, axis, offset):
    at = list(offset)
    at[axis] = (at[axis] - 1) % dims[axis]
    return tuple(at)


def gather_plan(dims):
    if dims == (4, 2, 2):
        return [
            [((0, 0, 1), 2), ((0, 1, 0), 1), ((1, 0, 0), 0)],
            [((2, 0, 0), 0), ((0, 1, 1), 2), ((1, 1, 0), 1)],
            [((3, 0, 0), 0), ((1, 1, 1), 2), ((2, 1, 0), 1)],
            [((3, 0, 1), 2), ((3, 1, 0), 1), ((1, 0, 1), 0)],
            [((2, 1, 1), 2), ((3, 1, 1), 1), ((2, 0, 1), 0)],
        ]
    total = 1
    for size in dims:
        total *= size
    held = {(0,) * len(dims)}
    slots = []
    while len(held) < total:
        slot = []
        taken = set()
        for axis in range(len(dims)):
            for index in range(1, total):
                offset = unflat(dims, index)
                if offset not in held and offset not in taken and back(dims, axis, offset) in held:
                    slot.append((offset, axis))
                    taken.add(offset)
                    break
        held |= taken
        slots.append(slot)
    return slots


def pack_kernel(rows_ref, cols_ref, counts_ref, tiles_ref, unit_ref, sem):
    steps, _, per_dev = rows_ref.shape
    body = tiles_ref.shape[0]
    copy = pltpu.make_async_copy(tiles_ref, unit_ref.at[pl.ds(0, body)], sem)
    copy.start()
    lane = lax.broadcasted_iota(jnp.int32, (META, 128), 1)
    meta = jnp.zeros((META, 128), jnp.int32)
    n_slots = steps * per_dev
    for step in range(steps):
        for q in range(per_dev):
            at = step * per_dev + q
            row = jnp.where(q < counts_ref[step, 0, 0], rows_ref[step, 0, q], RB_DEV)
            meta = jnp.where(lane == at, row, meta)
            meta = jnp.where(lane == n_slots + at, cols_ref[step, 0, q], meta)
    unit_ref[pl.ds(body, META), :] = meta.astype(jnp.float32).astype(jnp.bfloat16)
    copy.wait()


def pack(rows, cols, counts, tiles):
    steps, _, per_dev, size, _ = tiles.shape
    body = steps * per_dev * size
    smem = pl.BlockSpec(memory_space=pltpu.SMEM)
    return pl.pallas_call(
        pack_kernel,
        out_shape=jax.ShapeDtypeStruct((body + META, size), jnp.bfloat16),
        in_specs=[smem, smem, smem, pl.BlockSpec(memory_space=pl.ANY)],
        out_specs=pl.BlockSpec(memory_space=pltpu.VMEM),
        scratch_shapes=[pltpu.SemaphoreType.DMA],
        compiler_params=pltpu.CompilerParams(vmem_limit_bytes=2 << 20),
        name="pack",
    )(rows, cols, counts, tiles.reshape(body, size))


def panel_kernel(*refs, n_row):
    pieces, whole_ref, acc_ref, sem = refs[:n_row], refs[n_row], refs[n_row + 1], refs[n_row + 2]
    steps, depth, _ = pieces[0].shape
    me = lax.axis_index("row")
    copies = []
    for back_by, piece in enumerate(pieces):
        owner = lax.rem(me - back_by + n_row, n_row)
        for step in range(steps):
            copies.append(
                pltpu.make_async_copy(
                    piece.at[step],
                    whole_ref.at[step, pl.ds(owner * depth, depth)],
                    sem.at[back_by * steps + step],
                )
            )
    for copy in copies:
        copy.start()
    acc_ref[...] = jnp.zeros_like(acc_ref)
    for copy in copies:
        copy.wait()


def whole_panels(pieces, size):
    n_row = len(pieces)
    steps, depth, scen = pieces[0].shape
    return pl.pallas_call(
        functools.partial(panel_kernel, n_row=n_row),
        out_shape=(
            pltpu.VMEM((steps, n_row * depth, scen), jnp.bfloat16),
            pltpu.VMEM(((RB_DEV + 1) * size, scen), jnp.float32),
        ),
        in_specs=[pl.BlockSpec(memory_space=pl.ANY)] * n_row,
        out_specs=(pl.BlockSpec(memory_space=pltpu.VMEM),) * 2,
        scratch_shapes=[pltpu.SemaphoreType.DMA((n_row * steps,))],
        compiler_params=pltpu.CompilerParams(vmem_limit_bytes=2 << 20),
        name="panels",
    )(*pieces)


def add_units(n, steps, size, unit_refs, panel_ref, acc_ref, meta_ref, index_ref, sem):
    body = unit_refs[0].shape[0] - META
    n_slots = body // size
    per_step = n_slots // steps
    for k in range(n):
        meta = unit_refs[k][pl.ds(body, META), :].astype(jnp.float32).astype(jnp.int32)
        meta_ref[pl.ds(8 * k, 8), :] = meta[:8]
    copy = pltpu.make_async_copy(meta_ref, index_ref, sem)
    copy.start()
    copy.wait()
    for k in range(n):
        for q in range(n_slots):
            row = index_ref[8 * k, q]
            col = index_ref[8 * k, n_slots + q]
            product = jnp.dot(
                unit_refs[k][pl.ds(q * size, size), :],
                panel_ref[q // per_step, pl.ds(pl.multiple_of(col * size, size), size), :],
                preferred_element_type=jnp.float32,
            )
            at = pl.ds(pl.multiple_of(row * size, size), size)
            acc_ref[at, :] = acc_ref[at, :] + product


def fold_kernel(*refs, n, steps, size):
    unit_refs, panel_ref, _, acc_ref, meta_ref, index_ref, sem = refs[:n], *refs[n:]
    add_units(n, steps, size, unit_refs, panel_ref, acc_ref, meta_ref, index_ref, sem)


def last_kernel(*refs, n, steps, size):
    unit_refs, panel_ref, _, acc_ref, out_ref, meta_ref, index_ref, sem, out_sem = refs[:n], *refs[n:]
    add_units(n, steps, size, unit_refs, panel_ref, acc_ref, meta_ref, index_ref, sem)
    copy = pltpu.make_async_copy(acc_ref.at[pl.ds(0, out_ref.shape[0])], out_ref, out_sem)
    copy.start()
    copy.wait()


def fold(units, panels, acc, last):
    n = len(units)
    steps = panels.shape[0]
    rows, size = units[0].shape
    scen = panels.shape[2]
    vmem = pl.BlockSpec(memory_space=pltpu.VMEM)
    acc_shape = pltpu.VMEM(acc.shape, jnp.float32)
    scratch = [
        pltpu.VMEM((8 * n, 128), jnp.int32),
        pltpu.SMEM((8 * n, 128), jnp.int32),
        pltpu.SemaphoreType.DMA,
    ]
    cost = pl.CostEstimate(
        flops=2 * n * (rows - META) * size * scen, bytes_accessed=n * rows * size * 2, transcendentals=0
    )
    if last:
        _, out = pl.pallas_call(
            functools.partial(last_kernel, n=n, steps=steps, size=size),
            out_shape=(acc_shape, jax.ShapeDtypeStruct((RB_DEV * size, scen), jnp.float32)),
            in_specs=[vmem] * (n + 2),
            out_specs=(vmem, pl.BlockSpec(memory_space=pl.ANY)),
            input_output_aliases={n + 1: 0},
            scratch_shapes=scratch + [pltpu.SemaphoreType.DMA],
            cost_estimate=cost,
            compiler_params=pltpu.CompilerParams(vmem_limit_bytes=8 << 20),
            name="last",
        )(*units, panels, acc)
        return out
    return pl.pallas_call(
        functools.partial(fold_kernel, n=n, steps=steps, size=size),
        out_shape=acc_shape,
        in_specs=[vmem] * (n + 2),
        out_specs=vmem,
        input_output_aliases={n + 1: 0},
        scratch_shapes=scratch,
        cost_estimate=cost,
        compiler_params=pltpu.CompilerParams(vmem_limit_bytes=8 << 20),
        name="fold",
    )(*units, panels, acc)


def per_device(tiles, block_rows, block_cols, live_counts, panels, n_row, n_col):
    size = tiles.shape[3]
    dims = col_dims(n_col)
    ring = [(i, (i + 1) % n_row) for i in range(n_row)]
    pieces = [panels]
    for _ in range(n_row - 1):
        pieces.append(lax.ppermute(pieces[-1], "row", ring))
    own = pack(block_rows, block_cols, live_counts, tiles)
    held = {(0,) * len(dims): own}
    waiting = [own]
    acc = None
    for slot in gather_plan(dims):
        arrived = tuple(hop(dims, axis, held[back(dims, axis, offset)]) for offset, axis in slot)
        if acc is None:
            whole, acc = whole_panels(pieces, size)
        acc = fold(waiting, whole, acc, False)
        arrived = lax.optimization_barrier(arrived)
        for (offset, _), unit in zip(slot, arrived):
            held[offset] = unit
        waiting = list(arrived)
    return fold(waiting, whole, acc, True)


def solution(mesh):
    placed = (
        P(None, "row", "col", None, None),
        P(None, "row", "col"),
        P(None, "row", "col"),
        P(None, "row", "col"),
        P(None, "row", "col"),
    )
    body = functools.partial(per_device, n_row=mesh.shape["row"], n_col=mesh.shape["col"])
    return jax.shard_map(body, mesh=mesh, in_specs=placed, out_specs=P("row", "col"), check_vma=False)
```

```python
import functools

import jax
import jax.numpy as jnp
from jax import lax
from jax.experimental import pallas as pl
from jax.experimental.pallas import tpu as pltpu
from jax.sharding import PartitionSpec as P

RB_DEV = 32
META = 16


def col_dims(n_col):
    return (4, 2, n_col // 8) if n_col % 8 == 0 else (n_col,)


def flat(dims, offset):
    index = 0
    for size, part in zip(dims, offset):
        index = index * size + part % size
    return index


def unflat(dims, index):
    parts = []
    for size in reversed(dims):
        parts.append(index % size)
        index //= size
    return tuple(reversed(parts))


def hop(dims, axis, sign, unit):
    n_col = 1
    for size in dims:
        n_col *= size
    size = dims[axis]
    pairs = []
    for index in range(n_col):
        at = list(unflat(dims, index))
        at[axis] = (at[axis] + sign) % size
        pairs.append((index, flat(dims, at)))
    return lax.ppermute(unit, "col", pairs)


def source(dims, offset, axis, sign):
    at = list(offset)
    at[axis] = (at[axis] - sign) % dims[axis]
    return tuple(at)


def gather_plan(dims):
    if dims == (4, 2, 2):
        return [
            ((1, 0, 0), 0, 1),
            ((0, 1, 0), 1, 1),
            ((0, 0, 1), 2, 1),
            [(0, 0, 0)],
            ((3, 0, 0), 0, -1),
            ((1, 0, 1), 2, 1),
            ((1, 1, 0), 1, 1),
            ((2, 0, 0), 0, 1),
            [(1, 0, 0), (0, 1, 0), (0, 0, 1)],
            ((3, 0, 1), 2, 1),
            ((3, 1, 0), 1, 1),
            ((2, 0, 1), 0, 1),
            ((1, 1, 1), 2, 1),
            ((0, 1, 1), 1, 1),
            ((2, 1, 0), 0, 1),
            [(3, 0, 0), (1, 0, 1), (1, 1, 0)],
            ((3, 1, 1), 2, 1),
            [(2, 0, 0), (3, 0, 1), (3, 1, 0)],
            ((2, 1, 1), 1, 1),
            [(2, 0, 1), (1, 1, 1), (0, 1, 1)],
        ]
    total = 1
    for size in dims:
        total *= size
    held = {(0,) * len(dims)}
    plan = []
    ready = list(held)
    while len(held) < total:
        taken = []
        for axis in range(len(dims)):
            for index in range(1, total):
                offset = unflat(dims, index)
                if offset not in held and offset not in taken and source(dims, offset, axis, 1) in held:
                    plan.append((offset, axis, 1))
                    taken.append(offset)
                    break
        plan.append(ready)
        held.update(taken)
        ready = taken
    return plan


def pack_kernel(rows_hbm, cols_hbm, counts_hbm, tiles_ref, unit_ref, rows_ref, cols_ref, counts_ref, sem):
    steps, _, per_dev = rows_ref.shape
    body = tiles_ref.shape[0]
    copies = [
        pltpu.make_async_copy(tiles_ref, unit_ref.at[pl.ds(0, body)], sem.at[0]),
        pltpu.make_async_copy(rows_hbm, rows_ref, sem.at[1]),
        pltpu.make_async_copy(cols_hbm, cols_ref, sem.at[2]),
        pltpu.make_async_copy(counts_hbm, counts_ref, sem.at[3]),
    ]
    for copy in copies:
        copy.start()
    for copy in copies[1:]:
        copy.wait()
    lane = lax.broadcasted_iota(jnp.int32, (META, 128), 1)
    meta = jnp.zeros((META, 128), jnp.int32)
    n_slots = steps * per_dev
    for step in range(steps):
        for q in range(per_dev):
            at = step * per_dev + q
            row = jnp.where(q < counts_ref[step], rows_ref[step, 0, q], RB_DEV)
            meta = jnp.where(lane == at, row, meta)
            meta = jnp.where(lane == n_slots + at, cols_ref[step, 0, q], meta)
    unit_ref[pl.ds(body, META), :] = meta.astype(jnp.float32).astype(jnp.bfloat16)
    copies[0].wait()


def pack(rows, cols, counts, tiles):
    steps, _, per_dev, size, _ = tiles.shape
    body = steps * per_dev * size
    return pl.pallas_call(
        pack_kernel,
        out_shape=jax.ShapeDtypeStruct((body + META, size), jnp.bfloat16),
        in_specs=[pl.BlockSpec(memory_space=pltpu.HBM)] * 4,
        out_specs=pl.BlockSpec(memory_space=pltpu.VMEM),
        scratch_shapes=[
            pltpu.SMEM(rows.shape, jnp.int32),
            pltpu.SMEM(cols.shape, jnp.int32),
            pltpu.SMEM((steps,), jnp.int32),
            pltpu.SemaphoreType.DMA((4,)),
        ],
        compiler_params=pltpu.CompilerParams(vmem_limit_bytes=2 << 20),
        name="pack",
    )(*(pltpu.with_memory_space_constraint(x, pltpu.HBM) for x in (rows, cols, counts.reshape(steps), tiles.reshape(body, size))))


def panel_kernel(*refs, n_row):
    pieces, whole_ref, acc_ref, sem = refs[:n_row], refs[n_row], refs[n_row + 1], refs[n_row + 2]
    steps, depth, _ = pieces[0].shape
    me = lax.axis_index("row")
    copies = []
    for back_by, piece in enumerate(pieces):
        owner = lax.rem(me - back_by + n_row, n_row)
        for step in range(steps):
            copies.append(
                pltpu.make_async_copy(
                    piece.at[step],
                    whole_ref.at[step, pl.ds(owner * depth, depth)],
                    sem.at[back_by * steps + step],
                )
            )
    for copy in copies:
        copy.start()
    acc_ref[...] = jnp.zeros_like(acc_ref)
    for copy in copies:
        copy.wait()


def whole_panels(pieces, size):
    n_row = len(pieces)
    steps, depth, scen = pieces[0].shape
    return pl.pallas_call(
        functools.partial(panel_kernel, n_row=n_row),
        out_shape=(
            pltpu.VMEM((steps, n_row * depth, scen), jnp.bfloat16),
            pltpu.VMEM(((RB_DEV + 1) * size, scen), jnp.float32),
        ),
        in_specs=[pl.BlockSpec(memory_space=pltpu.HBM)] + [pl.BlockSpec(memory_space=pl.ANY)] * (n_row - 1),
        out_specs=(pl.BlockSpec(memory_space=pltpu.VMEM),) * 2,
        scratch_shapes=[pltpu.SemaphoreType.DMA((n_row * steps,))],
        compiler_params=pltpu.CompilerParams(vmem_limit_bytes=2 << 20),
        name="panels",
    )(pltpu.with_memory_space_constraint(pieces[0], pltpu.HBM), *pieces[1:])


def add_units(n, steps, size, unit_refs, panel_ref, acc_ref, meta_ref, index_ref, sem):
    body = unit_refs[0].shape[0] - META
    n_slots = body // size
    per_step = n_slots // steps
    for k in range(n):
        meta = unit_refs[k][pl.ds(body, META), :].astype(jnp.float32).astype(jnp.int32)
        meta_ref[pl.ds(8 * k, 8), :] = meta[:8]
    copy = pltpu.make_async_copy(meta_ref, index_ref, sem)
    copy.start()
    copy.wait()
    for k in range(n):
        for q in range(n_slots):
            row = index_ref[8 * k, q]
            col = index_ref[8 * k, n_slots + q]
            product = jnp.dot(
                unit_refs[k][pl.ds(q * size, size), :],
                panel_ref[q // per_step, pl.ds(pl.multiple_of(col * size, size), size), :],
                preferred_element_type=jnp.float32,
            )
            at = pl.ds(pl.multiple_of(row * size, size), size)
            acc_ref[at, :] = acc_ref[at, :] + product


def fold_kernel(*refs, n, steps, size):
    unit_refs, panel_ref, _, acc_ref, meta_ref, index_ref, sem = refs[:n], *refs[n:]
    add_units(n, steps, size, unit_refs, panel_ref, acc_ref, meta_ref, index_ref, sem)


def last_kernel(*refs, n, steps, size):
    unit_refs, panel_ref, _, acc_ref, out_ref, meta_ref, index_ref, sem, out_sem = refs[:n], *refs[n:]
    add_units(n, steps, size, unit_refs, panel_ref, acc_ref, meta_ref, index_ref, sem)
    copy = pltpu.make_async_copy(acc_ref.at[pl.ds(0, out_ref.shape[0])], out_ref, out_sem)
    copy.start()
    copy.wait()


def fold(units, panels, acc, last):
    n = len(units)
    steps = panels.shape[0]
    rows, size = units[0].shape
    scen = panels.shape[2]
    vmem = pl.BlockSpec(memory_space=pltpu.VMEM)
    acc_shape = pltpu.VMEM(acc.shape, jnp.float32)
    scratch = [
        pltpu.VMEM((8 * n, 128), jnp.int32),
        pltpu.SMEM((8 * n, 128), jnp.int32),
        pltpu.SemaphoreType.DMA,
    ]
    cost = pl.CostEstimate(
        flops=2 * n * (rows - META) * size * scen, bytes_accessed=n * rows * size * 2, transcendentals=0
    )
    if last:
        _, out = pl.pallas_call(
            functools.partial(last_kernel, n=n, steps=steps, size=size),
            out_shape=(acc_shape, jax.ShapeDtypeStruct((RB_DEV * size, scen), jnp.float32)),
            in_specs=[vmem] * (n + 2),
            out_specs=(vmem, pl.BlockSpec(memory_space=pl.ANY)),
            input_output_aliases={n + 1: 0},
            scratch_shapes=scratch + [pltpu.SemaphoreType.DMA],
            cost_estimate=cost,
            compiler_params=pltpu.CompilerParams(vmem_limit_bytes=8 << 20),
            name="last",
        )(*units, panels, acc)
        return out
    return pl.pallas_call(
        functools.partial(fold_kernel, n=n, steps=steps, size=size),
        out_shape=acc_shape,
        in_specs=[vmem] * (n + 2),
        out_specs=vmem,
        input_output_aliases={n + 1: 0},
        scratch_shapes=scratch,
        cost_estimate=cost,
        compiler_params=pltpu.CompilerParams(vmem_limit_bytes=8 << 20),
        name="fold",
    )(*units, panels, acc)


def per_device(tiles, block_rows, block_cols, live_counts, panels, n_row, n_col):
    size = tiles.shape[3]
    dims = col_dims(n_col)
    ring = [(i, (i + 1) % n_row) for i in range(n_row)]
    pieces = [panels]
    for _ in range(n_row - 1):
        pieces.append(lax.ppermute(pieces[-1], "row", ring))
    own = pack(block_rows, block_cols, live_counts, tiles)
    held = {(0,) * len(dims): own}
    seen = set(held)
    folded = set()
    whole, acc = whole_panels(pieces, size)
    for step in gather_plan(dims):
        if isinstance(step, list):
            acc = fold([held[key] for key in step], whole, acc, False)
            folded.update(step)
            continue
        offset, axis, sign = step
        origin = source(dims, offset, axis, sign)
        seen.add(origin)
        keys = [key for key in held if key in seen]
        if folded:
            *tied, acc = lax.optimization_barrier((*(held[key] for key in keys), acc))
            held.update(zip(keys, tied))
        held[offset] = hop(dims, axis, sign, held[origin])
    return fold([held[key] for key in held if key not in folded], whole, acc, True)


def solution(mesh):
    placed = (
        P(None, "row", "col", None, None),
        P(None, "row", "col"),
        P(None, "row", "col"),
        P(None, "row", "col"),
        P(None, "row", "col"),
    )
    body = functools.partial(per_device, n_row=mesh.shape["row"], n_col=mesh.shape["col"])
    return jax.shard_map(body, mesh=mesh, in_specs=placed, out_specs=P("row", "col"), check_vma=False)
```

```python
import functools

import jax
import jax.numpy as jnp
from jax import lax
from jax.experimental import pallas as pl
from jax.experimental.pallas import tpu as pltpu
from jax.sharding import PartitionSpec as P

RB_DEV = 32
META = 16


PARTS = ((0, 12),)
PLAN = [
    (0, 1, 0),
    (0, 12, 3),
    (0, 2, 1),
    [(0, 0)],
    (0, 5, 2),
    (0, 13, 0),
    (0, 14, 1),
    (0, 6, 2),
    [(0, 1), (0, 12), (0, 2)],
    (0, 3, 0),
    (0, 7, 1),
    (0, 9, 2),
    [(0, 5), (0, 13)],
    (0, 4, 0),
    (0, 15, 1),
    (0, 10, 2),
    [(0, 14), (0, 6), (0, 3)],
    (0, 8, 0),
    (0, 11, 1),
    [(0, 9), (0, 7)],
    [(0, 4)],
    [(0, 15)],
]


def ring_of(n_col):
    return (0, 1, 3, 2) if n_col == 16 else tuple(range(n_col // 4))


def moved(n_col, index, direction):
    if direction < 2:
        return index ^ (1 + direction)
    ring = ring_of(n_col)
    at = ring.index(index // 4) + (1 if direction == 2 else -1)
    return ring[at % len(ring)] * 4 + index % 4


def hop(n_row, n_col, direction, unit):
    pairs = []
    for row in range(n_row):
        way = direction ^ 1 if row % 2 and direction < 2 else direction
        pairs += [(row * n_col + i, row * n_col + moved(n_col, i, way)) for i in range(n_col)]
    return lax.ppermute(unit, ("row", "col"), pairs)


def origin(n_col, key, direction):
    return (key ^ 1, key ^ 2, (key - 4) % n_col, (key + 4) % n_col)[direction]


def gather_plan(n_col, n_slots):
    if n_col == 16 and n_slots == PARTS[-1][1]:
        return PARTS, PLAN
    steps = []
    held = [0]
    ready = [(0, 0)]
    while len(held) < n_col:
        taken = []
        for direction in range(3):
            for key in range(1, n_col):
                if key not in held and key not in taken and origin(n_col, key, direction) in held:
                    steps.append((0, key, direction))
                    taken.append(key)
                    break
        steps.append(ready)
        held += taken
        ready = [(0, key) for key in taken]
    return ((0, n_slots),), steps


def pack_kernel(rows_hbm, cols_hbm, counts_hbm, tiles_ref, *refs, parts, size):
    unit_refs, (rows_ref, cols_ref, counts_ref, sem) = refs[: len(parts)], refs[len(parts) :]
    per_dev = rows_ref.shape[2]
    copies = [
        pltpu.make_async_copy(rows_hbm, rows_ref, sem.at[0]),
        pltpu.make_async_copy(cols_hbm, cols_ref, sem.at[1]),
        pltpu.make_async_copy(counts_hbm, counts_ref, sem.at[2]),
    ]
    for p, (low, high) in enumerate(parts):
        here = tiles_ref.at[pl.ds(low * size, (high - low) * size)]
        copies.append(pltpu.make_async_copy(here, unit_refs[p].at[pl.ds(0, (high - low) * size)], sem.at[3 + p]))
    for copy in copies:
        copy.start()
    for copy in copies[:3]:
        copy.wait()
    lane = lax.broadcasted_iota(jnp.int32, (META, 128), 1)
    for p, (low, high) in enumerate(parts):
        meta = jnp.zeros((META, 128), jnp.int32)
        for slot in range(low, high):
            step, q = slot // per_dev, slot % per_dev
            row = jnp.where(q < counts_ref[step], rows_ref[step, 0, q], RB_DEV)
            meta = jnp.where(lane == slot - low, row, meta)
            meta = jnp.where(lane == high - 2 * low + slot, cols_ref[step, 0, q], meta)
        unit_refs[p][pl.ds((high - low) * size, META), :] = meta.astype(jnp.float32).astype(jnp.bfloat16)
    for copy in copies[3:]:
        copy.wait()


def pack(rows, cols, counts, tiles, parts):
    steps, _, per_dev, size, _ = tiles.shape
    args = rows, cols, counts.reshape(steps), tiles.reshape(steps * per_dev * size, size)
    return pl.pallas_call(
        functools.partial(pack_kernel, parts=parts, size=size),
        out_shape=tuple(jax.ShapeDtypeStruct(((high - low) * size + META, size), jnp.bfloat16) for low, high in parts),
        in_specs=[pl.BlockSpec(memory_space=pltpu.HBM)] * 4,
        out_specs=(pl.BlockSpec(memory_space=pltpu.VMEM),) * len(parts),
        scratch_shapes=[
            pltpu.SMEM(rows.shape, jnp.int32),
            pltpu.SMEM(cols.shape, jnp.int32),
            pltpu.SMEM((steps,), jnp.int32),
            pltpu.SemaphoreType.DMA((3 + len(parts),)),
        ],
        compiler_params=pltpu.CompilerParams(vmem_limit_bytes=2 << 20),
        name="pack",
    )(*(pltpu.with_memory_space_constraint(x, pltpu.HBM) for x in args))


def panel_kernel(*refs, n_row):
    pieces, whole_ref, acc_ref, sem = refs[:n_row], refs[n_row], refs[n_row + 1], refs[n_row + 2]
    steps, depth, _ = pieces[0].shape
    me = lax.axis_index("row")
    copies = []
    for back_by, piece in enumerate(pieces):
        owner = lax.rem(me - back_by + n_row, n_row)
        for step in range(steps):
            copies.append(
                pltpu.make_async_copy(
                    piece.at[step],
                    whole_ref.at[step, pl.ds(owner * depth, depth)],
                    sem.at[back_by * steps + step],
                )
            )
    for copy in copies:
        copy.start()
    acc_ref[...] = jnp.zeros_like(acc_ref)
    for copy in copies:
        copy.wait()


def whole_panels(pieces, size):
    n_row = len(pieces)
    steps, depth, scen = pieces[0].shape
    return pl.pallas_call(
        functools.partial(panel_kernel, n_row=n_row),
        out_shape=(
            pltpu.VMEM((steps, n_row * depth, scen), jnp.bfloat16),
            pltpu.VMEM(((RB_DEV + 1) * size, scen), jnp.float32),
        ),
        in_specs=[pl.BlockSpec(memory_space=pltpu.HBM)] + [pl.BlockSpec(memory_space=pl.ANY)] * (n_row - 1),
        out_specs=(pl.BlockSpec(memory_space=pltpu.VMEM),) * 2,
        scratch_shapes=[pltpu.SemaphoreType.DMA((n_row * steps,))],
        compiler_params=pltpu.CompilerParams(vmem_limit_bytes=2 << 20),
        name="panels",
    )(pltpu.with_memory_space_constraint(pieces[0], pltpu.HBM), *pieces[1:])


def add_units(slots, size, unit_refs, panel_ref, acc_ref, meta_ref, index_ref, sem):
    for k, unit_ref in enumerate(unit_refs):
        meta = unit_ref[pl.ds(len(slots[k]) * size, META), :].astype(jnp.float32).astype(jnp.int32)
        meta_ref[pl.ds(8 * k, 8), :] = meta[:8]
    copy = pltpu.make_async_copy(meta_ref, index_ref, sem)
    copy.start()
    copy.wait()
    for k, unit_ref in enumerate(unit_refs):
        for q, step in enumerate(slots[k]):
            row = index_ref[8 * k, q]
            col = index_ref[8 * k, len(slots[k]) + q]
            product = jnp.dot(
                unit_ref[pl.ds(q * size, size), :],
                panel_ref[step, pl.ds(pl.multiple_of(col * size, size), size), :],
                preferred_element_type=jnp.float32,
            )
            at = pl.ds(pl.multiple_of(row * size, size), size)
            acc_ref[at, :] = acc_ref[at, :] + product


def fold_kernel(*refs, slots, size):
    n = len(slots)
    unit_refs, (panel_ref, _, acc_ref, meta_ref, index_ref, sem) = refs[:n], refs[n:]
    add_units(slots, size, unit_refs, panel_ref, acc_ref, meta_ref, index_ref, sem)


def last_kernel(*refs, slots, size):
    n = len(slots)
    unit_refs, (panel_ref, _, acc_ref, out_ref, meta_ref, index_ref, sem, out_sem) = refs[:n], refs[n:]
    add_units(slots, size, unit_refs, panel_ref, acc_ref, meta_ref, index_ref, sem)
    copy = pltpu.make_async_copy(acc_ref.at[pl.ds(0, out_ref.shape[0])], out_ref, out_sem)
    copy.start()
    copy.wait()


def fold(units, slots, panels, acc, last):
    n = len(units)
    size = units[0].shape[1]
    scen = panels.shape[2]
    vmem = pl.BlockSpec(memory_space=pltpu.VMEM)
    out_shape = [pltpu.VMEM(acc.shape, jnp.float32)]
    out_specs = [vmem]
    scratch = [pltpu.VMEM((8 * n, 128), jnp.int32), pltpu.SMEM((8 * n, 128), jnp.int32), pltpu.SemaphoreType.DMA]
    if last:
        out_shape.append(jax.ShapeDtypeStruct((RB_DEV * size, scen), jnp.float32))
        out_specs.append(pl.BlockSpec(memory_space=pltpu.HBM))
        scratch.append(pltpu.SemaphoreType.DMA)
    tiles = sum(len(held) for held in slots)
    return pl.pallas_call(
        functools.partial(last_kernel if last else fold_kernel, slots=slots, size=size),
        out_shape=tuple(out_shape),
        in_specs=[vmem] * (n + 2),
        out_specs=tuple(out_specs),
        input_output_aliases={n + 1: 0},
        scratch_shapes=scratch,
        compiler_params=pltpu.CompilerParams(vmem_limit_bytes=8 << 20),
        cost_estimate=pl.CostEstimate(
            flops=2 * tiles * size * size * scen, bytes_accessed=2 * tiles * size * size, transcendentals=0
        ),
        name="last" if last else "fold",
    )(*units, panels, acc)[-1]


def per_device(tiles, block_rows, block_cols, live_counts, panels, n_row, n_col):
    steps, _, per_dev, size, _ = tiles.shape
    parts, plan = gather_plan(n_col, steps * per_dev)
    slots = [[slot // per_dev for slot in range(low, high)] for low, high in parts]
    ring = [(i, (i + 1) % n_row) for i in range(n_row)]
    pieces = [panels]
    for _ in range(n_row - 1):
        pieces.append(lax.ppermute(pieces[-1], "row", ring))
    held = {(p, 0): unit for p, unit in enumerate(pack(block_rows, block_cols, live_counts, tiles, parts))}
    seen = set(held)
    folded = set()
    whole, acc = whole_panels(pieces, size)
    for step in plan:
        if isinstance(step, list):
            acc = fold([held[name] for name in step], [slots[p] for p, _ in step], whole, acc, False)
            folded.update(step)
            continue
        p, key, direction = step
        source = (p, origin(n_col, key, direction))
        seen.add(source)
        if folded:
            names = [name for name in held if name in seen]
            *tied, acc = lax.optimization_barrier((*(held[name] for name in names), acc))
            held.update(zip(names, tied))
        held[p, key] = hop(n_row, n_col, direction, held[source])
    rest = [name for name in held if name not in folded]
    return fold([held[name] for name in rest], [slots[p] for p, _ in rest], whole, acc, True)


def solution(mesh):
    placed = (
        P(None, "row", "col", None, None),
        P(None, "row", "col"),
        P(None, "row", "col"),
        P(None, "row", "col"),
        P(None, "row", "col"),
    )
    body = functools.partial(per_device, n_row=mesh.shape["row"], n_col=mesh.shape["col"])
    return jax.shard_map(body, mesh=mesh, in_specs=placed, out_specs=P("row", "col"), check_vma=False)
```

```python
import functools

import jax
import jax.numpy as jnp
from jax import lax
from jax.experimental import pallas as pl
from jax.experimental.pallas import tpu as pltpu
from jax.sharding import PartitionSpec as P

RB_DEV = 32
META = 16


PARTS = ((0, 12),)
PLAN = [
    (0, 1, 0),
    (0, 12, 3),
    (0, 2, 1),
    [(0, 0)],
    (0, 5, 2),
    (0, 14, 1),
    (0, 13, 0),
    (0, 6, 2),
    [(0, 1), (0, 12), (0, 2)],
    (0, 3, 1),
    (0, 4, 0),
    [(0, 5)],
    (0, 9, 2),
    [(0, 14)],
    (0, 7, 1),
    [(0, 13)],
    (0, 15, 0),
    (0, 10, 2),
    [(0, 6), (0, 3)],
    (0, 11, 1),
    (0, 8, 0),
    [(0, 9), (0, 4)],
    [(0, 7)],
    [(0, 15)],
]


def ring_of(n_col):
    return (0, 1, 3, 2) if n_col == 16 else tuple(range(n_col // 4))


def moved(n_col, index, direction):
    if direction < 2:
        return index ^ (1 + direction)
    ring = ring_of(n_col)
    at = ring.index(index // 4) + (1 if direction == 2 else -1)
    return ring[at % len(ring)] * 4 + index % 4


def hop(n_row, n_col, direction, unit):
    pairs = []
    for row in range(n_row):
        way = direction ^ 1 if row % 2 and direction < 2 else direction
        pairs += [(row * n_col + i, row * n_col + moved(n_col, i, way)) for i in range(n_col)]
    return lax.ppermute(unit, ("row", "col"), pairs)


def origin(n_col, key, direction):
    return (key ^ 1, key ^ 2, (key - 4) % n_col, (key + 4) % n_col)[direction]


def gather_plan(n_col, n_slots):
    if n_col == 16 and n_slots == PARTS[-1][1]:
        return PARTS, PLAN
    steps = []
    held = [0]
    ready = [(0, 0)]
    while len(held) < n_col:
        taken = []
        for direction in range(3):
            for key in range(1, n_col):
                if key not in held and key not in taken and origin(n_col, key, direction) in held:
                    steps.append((0, key, direction))
                    taken.append(key)
                    break
        steps.append(ready)
        held += taken
        ready = [(0, key) for key in taken]
    return ((0, n_slots),), steps


def pack_kernel(rows_hbm, cols_hbm, counts_hbm, tiles_ref, *refs, parts, size):
    unit_refs, (rows_ref, cols_ref, counts_ref, sem) = refs[: len(parts)], refs[len(parts) :]
    per_dev = rows_ref.shape[2]
    copies = [
        pltpu.make_async_copy(rows_hbm, rows_ref, sem.at[0]),
        pltpu.make_async_copy(cols_hbm, cols_ref, sem.at[1]),
        pltpu.make_async_copy(counts_hbm, counts_ref, sem.at[2]),
    ]
    for p, (low, high) in enumerate(parts):
        here = tiles_ref.at[pl.ds(low * size, (high - low) * size)]
        copies.append(pltpu.make_async_copy(here, unit_refs[p].at[pl.ds(0, (high - low) * size)], sem.at[3 + p]))
    for copy in copies:
        copy.start()
    for copy in copies[:3]:
        copy.wait()
    lane = lax.broadcasted_iota(jnp.int32, (META, 128), 1)
    for p, (low, high) in enumerate(parts):
        meta = jnp.zeros((META, 128), jnp.int32)
        for slot in range(low, high):
            step, q = slot // per_dev, slot % per_dev
            row = jnp.where(q < counts_ref[step], rows_ref[step, 0, q], RB_DEV)
            meta = jnp.where(lane == slot - low, row, meta)
            meta = jnp.where(lane == high - 2 * low + slot, cols_ref[step, 0, q], meta)
        unit_refs[p][pl.ds((high - low) * size, META), :] = meta.astype(jnp.float32).astype(jnp.bfloat16)
    for copy in copies[3:]:
        copy.wait()


def pack(rows, cols, counts, tiles, parts):
    steps, _, per_dev, size, _ = tiles.shape
    args = rows, cols, counts.reshape(steps), tiles.reshape(steps * per_dev * size, size)
    return pl.pallas_call(
        functools.partial(pack_kernel, parts=parts, size=size),
        out_shape=tuple(jax.ShapeDtypeStruct(((high - low) * size + META, size), jnp.bfloat16) for low, high in parts),
        in_specs=[pl.BlockSpec(memory_space=pltpu.HBM)] * 4,
        out_specs=(pl.BlockSpec(memory_space=pltpu.VMEM),) * len(parts),
        scratch_shapes=[
            pltpu.SMEM(rows.shape, jnp.int32),
            pltpu.SMEM(cols.shape, jnp.int32),
            pltpu.SMEM((steps,), jnp.int32),
            pltpu.SemaphoreType.DMA((3 + len(parts),)),
        ],
        compiler_params=pltpu.CompilerParams(vmem_limit_bytes=2 << 20),
        name="pack",
    )(*(pltpu.with_memory_space_constraint(x, pltpu.HBM) for x in args))


def panel_kernel(*refs, n_row):
    pieces, whole_ref, acc_ref, sem = refs[:n_row], refs[n_row], refs[n_row + 1], refs[n_row + 2]
    steps, depth, _ = pieces[0].shape
    me = lax.axis_index("row")
    copies = []
    for back_by, piece in enumerate(pieces):
        owner = lax.rem(me - back_by + n_row, n_row)
        for step in range(steps):
            copies.append(
                pltpu.make_async_copy(
                    piece.at[step],
                    whole_ref.at[step, pl.ds(owner * depth, depth)],
                    sem.at[back_by * steps + step],
                )
            )
    for copy in copies:
        copy.start()
    acc_ref[...] = jnp.zeros_like(acc_ref)
    for copy in copies:
        copy.wait()


def whole_panels(pieces, size):
    n_row = len(pieces)
    steps, depth, scen = pieces[0].shape
    return pl.pallas_call(
        functools.partial(panel_kernel, n_row=n_row),
        out_shape=(
            pltpu.VMEM((steps, n_row * depth, scen), jnp.bfloat16),
            pltpu.VMEM(((RB_DEV + 1) * size, scen), jnp.float32),
        ),
        in_specs=[pl.BlockSpec(memory_space=pltpu.HBM)] + [pl.BlockSpec(memory_space=pl.ANY)] * (n_row - 1),
        out_specs=(pl.BlockSpec(memory_space=pltpu.VMEM),) * 2,
        scratch_shapes=[pltpu.SemaphoreType.DMA((n_row * steps,))],
        compiler_params=pltpu.CompilerParams(vmem_limit_bytes=2 << 20),
        name="panels",
    )(pltpu.with_memory_space_constraint(pieces[0], pltpu.HBM), *pieces[1:])


def read_index(slots, size, unit_refs, meta_ref, index_ref, sem):
    for k, unit_ref in enumerate(unit_refs):
        meta = unit_ref[pl.ds(len(slots[k]) * size, META), :].astype(jnp.float32).astype(jnp.int32)
        meta_ref[pl.ds(8 * k, 8), :] = meta[:8]
    copy = pltpu.make_async_copy(meta_ref, index_ref, sem)
    copy.start()
    copy.wait()


def add_unit(k, slots, size, unit_ref, panel_ref, acc_ref, index_ref):
    for q, step in enumerate(slots[k]):
        row = index_ref[8 * k, q]
        col = index_ref[8 * k, len(slots[k]) + q]
        product = jnp.dot(
            unit_ref[pl.ds(q * size, size), :],
            panel_ref[step, pl.ds(pl.multiple_of(col * size, size), size), :],
            preferred_element_type=jnp.float32,
        )
        at = pl.ds(pl.multiple_of(row * size, size), size)
        acc_ref[at, :] = acc_ref[at, :] + product


def fold_kernel(*refs, slots, size):
    n = len(slots)
    unit_refs, (panel_ref, _, acc_ref, meta_ref, index_ref, sem) = refs[:n], refs[n:]
    read_index(slots, size, unit_refs, meta_ref, index_ref, sem)
    for k, unit_ref in enumerate(unit_refs):
        add_unit(k, slots, size, unit_ref, panel_ref, acc_ref, index_ref)


def last_kernel(*refs, slots, size):
    n = len(slots)
    unit_refs, (panel_ref, _, acc_ref, out_ref, meta_ref, index_ref, sem, out_sem) = refs[:n], refs[n:]
    read_index(slots, size, unit_refs, meta_ref, index_ref, sem)
    touched = [jnp.int32(0)]
    for k in reversed(range(n)):
        mask = touched[0]
        for q in range(len(slots[k])):
            row = index_ref[8 * k, q]
            mask = mask | jnp.where(row < RB_DEV, lax.shift_left(jnp.int32(1), row), 0)
        touched.insert(0, mask)

    def write(ready):
        for row in range(RB_DEV):
            at = pl.ds(row * size, size)

            @pl.when((lax.shift_right_logical(ready, jnp.int32(row)) & 1) == 1)
            def _():
                pltpu.make_async_copy(acc_ref.at[at], out_ref.at[at], out_sem).start()

    write(~touched[0])
    for k, unit_ref in enumerate(unit_refs):
        add_unit(k, slots, size, unit_ref, panel_ref, acc_ref, index_ref)
        write(touched[k] & ~touched[k + 1])
    pltpu.make_async_copy(acc_ref.at[pl.ds(0, out_ref.shape[0])], out_ref, out_sem).wait()


def fold(units, slots, panels, acc, last):
    n = len(units)
    size = units[0].shape[1]
    scen = panels.shape[2]
    vmem = pl.BlockSpec(memory_space=pltpu.VMEM)
    out_shape = [pltpu.VMEM(acc.shape, jnp.float32)]
    out_specs = [vmem]
    scratch = [pltpu.VMEM((8 * n, 128), jnp.int32), pltpu.SMEM((8 * n, 128), jnp.int32), pltpu.SemaphoreType.DMA]
    if last:
        out_shape.append(jax.ShapeDtypeStruct((RB_DEV * size, scen), jnp.float32))
        out_specs.append(pl.BlockSpec(memory_space=pltpu.HBM))
        scratch.append(pltpu.SemaphoreType.DMA)
    tiles = sum(len(held) for held in slots)
    return pl.pallas_call(
        functools.partial(last_kernel if last else fold_kernel, slots=slots, size=size),
        out_shape=tuple(out_shape),
        in_specs=[vmem] * (n + 2),
        out_specs=tuple(out_specs),
        input_output_aliases={n + 1: 0},
        scratch_shapes=scratch,
        compiler_params=pltpu.CompilerParams(vmem_limit_bytes=8 << 20),
        cost_estimate=pl.CostEstimate(
            flops=2 * tiles * size * size * scen, bytes_accessed=2 * tiles * size * size, transcendentals=0
        ),
        name="last" if last else "fold",
    )(*units, panels, acc)[-1]


def per_device(tiles, block_rows, block_cols, live_counts, panels, n_row, n_col):
    steps, _, per_dev, size, _ = tiles.shape
    parts, plan = gather_plan(n_col, steps * per_dev)
    slots = [[slot // per_dev for slot in range(low, high)] for low, high in parts]
    ring = [(i, (i + 1) % n_row) for i in range(n_row)]
    pieces = [panels]
    for _ in range(n_row - 1):
        pieces.append(lax.ppermute(pieces[-1], "row", ring))
    held = {(p, 0): unit for p, unit in enumerate(pack(block_rows, block_cols, live_counts, tiles, parts))}
    seen = set(held)
    folded = set()
    whole, acc = whole_panels(pieces, size)
    for step in plan:
        if isinstance(step, list):
            acc = fold([held[name] for name in step], [slots[p] for p, _ in step], whole, acc, False)
            folded.update(step)
            continue
        p, key, direction = step
        source = (p, origin(n_col, key, direction))
        seen.add(source)
        if folded:
            names = [name for name in held if name in seen]
            *tied, acc = lax.optimization_barrier((*(held[name] for name in names), acc))
            held.update(zip(names, tied))
        held[p, key] = hop(n_row, n_col, direction, held[source])
    rest = [name for name in held if name not in folded]
    return fold([held[name] for name in rest], [slots[p] for p, _ in rest], whole, acc, True)


def solution(mesh):
    placed = (
        P(None, "row", "col", None, None),
        P(None, "row", "col"),
        P(None, "row", "col"),
        P(None, "row", "col"),
        P(None, "row", "col"),
    )
    body = functools.partial(per_device, n_row=mesh.shape["row"], n_col=mesh.shape["col"])
    return jax.shard_map(body, mesh=mesh, in_specs=placed, out_specs=P("row", "col"), check_vma=False)
```

```python
import functools

import jax
import jax.numpy as jnp
from jax import lax
from jax.experimental import pallas as pl
from jax.experimental.pallas import tpu as pltpu
from jax.sharding import PartitionSpec as P

RB_DEV = 32
META = 16


PARTS = ((0, 12),)
PLAN = [
    (0, 1, 0),
    (0, 12, 3),
    (0, 2, 1),
    [(0, 0)],
    (0, 5, 2),
    (0, 14, 1),
    (0, 13, 0),
    (0, 6, 2),
    [(0, 1), (0, 12), (0, 2)],
    (0, 3, 1),
    (0, 4, 0),
    [(0, 5)],
    (0, 9, 2),
    [(0, 14)],
    (0, 7, 1),
    [(0, 13)],
    (0, 15, 0),
    (0, 10, 2),
    [(0, 6), (0, 3)],
    (0, 11, 1),
    (0, 8, 0),
    [(0, 9)],
    [(0, 4)],
    [(0, 7)],
    [(0, 15)],
]


def ring_of(n_col):
    return (0, 1, 3, 2) if n_col == 16 else tuple(range(n_col // 4))


def moved(n_col, index, direction):
    if direction < 2:
        return index ^ (1 + direction)
    ring = ring_of(n_col)
    at = ring.index(index // 4) + (1 if direction == 2 else -1)
    return ring[at % len(ring)] * 4 + index % 4


def hop(n_row, n_col, direction, unit):
    pairs = []
    for row in range(n_row):
        way = direction ^ 1 if row % 2 and direction < 2 else direction
        pairs += [(row * n_col + i, row * n_col + moved(n_col, i, way)) for i in range(n_col)]
    return lax.ppermute(unit, ("row", "col"), pairs)


def origin(n_col, key, direction):
    return (key ^ 1, key ^ 2, (key - 4) % n_col, (key + 4) % n_col)[direction]


def gather_plan(n_col, n_slots):
    if n_col == 16 and n_slots == PARTS[-1][1]:
        return PARTS, PLAN
    steps = []
    held = [0]
    ready = [(0, 0)]
    while len(held) < n_col:
        taken = []
        for direction in range(3):
            for key in range(1, n_col):
                if key not in held and key not in taken and origin(n_col, key, direction) in held:
                    steps.append((0, key, direction))
                    taken.append(key)
                    break
        steps.append(ready)
        held += taken
        ready = [(0, key) for key in taken]
    return ((0, n_slots),), steps


def pack_kernel(rows_hbm, cols_hbm, counts_hbm, tiles_ref, *refs, parts, size):
    unit_refs, (rows_ref, cols_ref, counts_ref, sem) = refs[: len(parts)], refs[len(parts) :]
    per_dev = rows_ref.shape[2]
    copies = [
        pltpu.make_async_copy(rows_hbm, rows_ref, sem.at[0]),
        pltpu.make_async_copy(cols_hbm, cols_ref, sem.at[1]),
        pltpu.make_async_copy(counts_hbm, counts_ref, sem.at[2]),
    ]
    for p, (low, high) in enumerate(parts):
        here = tiles_ref.at[pl.ds(low * size, (high - low) * size)]
        copies.append(pltpu.make_async_copy(here, unit_refs[p].at[pl.ds(0, (high - low) * size)], sem.at[3 + p]))
    for copy in copies:
        copy.start()
    for copy in copies[:3]:
        copy.wait()
    lane = lax.broadcasted_iota(jnp.int32, (META, 128), 1)
    for p, (low, high) in enumerate(parts):
        meta = jnp.zeros((META, 128), jnp.int32)
        for slot in range(low, high):
            step, q = slot // per_dev, slot % per_dev
            row = jnp.where(q < counts_ref[step], rows_ref[step, 0, q], RB_DEV)
            meta = jnp.where(lane == slot - low, row, meta)
            meta = jnp.where(lane == high - 2 * low + slot, cols_ref[step, 0, q], meta)
        unit_refs[p][pl.ds((high - low) * size, META), :] = meta.astype(jnp.float32).astype(jnp.bfloat16)
    for copy in copies[3:]:
        copy.wait()


def pack(rows, cols, counts, tiles, parts):
    steps, _, per_dev, size, _ = tiles.shape
    args = rows, cols, counts.reshape(steps), tiles.reshape(steps * per_dev * size, size)
    return pl.pallas_call(
        functools.partial(pack_kernel, parts=parts, size=size),
        out_shape=tuple(jax.ShapeDtypeStruct(((high - low) * size + META, size), jnp.bfloat16) for low, high in parts),
        in_specs=[pl.BlockSpec(memory_space=pltpu.HBM)] * 4,
        out_specs=(pl.BlockSpec(memory_space=pltpu.VMEM),) * len(parts),
        scratch_shapes=[
            pltpu.SMEM(rows.shape, jnp.int32),
            pltpu.SMEM(cols.shape, jnp.int32),
            pltpu.SMEM((steps,), jnp.int32),
            pltpu.SemaphoreType.DMA((3 + len(parts),)),
        ],
        compiler_params=pltpu.CompilerParams(vmem_limit_bytes=2 << 20),
        name="pack",
    )(*(pltpu.with_memory_space_constraint(x, pltpu.HBM) for x in args))


def panel_kernel(*refs, n_row):
    pieces, whole_ref, acc_ref, sem = refs[:n_row], refs[n_row], refs[n_row + 1], refs[n_row + 2]
    steps, depth, _ = pieces[0].shape
    me = lax.axis_index("row")
    copies = []
    for back_by, piece in enumerate(pieces):
        owner = lax.rem(me - back_by + n_row, n_row)
        for step in range(steps):
            copies.append(
                pltpu.make_async_copy(
                    piece.at[step],
                    whole_ref.at[step, pl.ds(owner * depth, depth)],
                    sem.at[back_by * steps + step],
                )
            )
    for copy in copies:
        copy.start()
    acc_ref[...] = jnp.zeros_like(acc_ref)
    for copy in copies:
        copy.wait()


def whole_panels(pieces, size):
    n_row = len(pieces)
    steps, depth, scen = pieces[0].shape
    return pl.pallas_call(
        functools.partial(panel_kernel, n_row=n_row),
        out_shape=(
            pltpu.VMEM((steps, n_row * depth, scen), jnp.bfloat16),
            pltpu.VMEM(((RB_DEV + 1) * size, scen), jnp.float32),
        ),
        in_specs=[pl.BlockSpec(memory_space=pltpu.HBM)] + [pl.BlockSpec(memory_space=pl.ANY)] * (n_row - 1),
        out_specs=(pl.BlockSpec(memory_space=pltpu.VMEM),) * 2,
        scratch_shapes=[pltpu.SemaphoreType.DMA((n_row * steps,))],
        compiler_params=pltpu.CompilerParams(vmem_limit_bytes=2 << 20),
        name="panels",
    )(pltpu.with_memory_space_constraint(pieces[0], pltpu.HBM), *pieces[1:])


def read_index(slots, size, unit_refs, meta_ref, index_ref, sem):
    for k, unit_ref in enumerate(unit_refs):
        meta = unit_ref[pl.ds(len(slots[k]) * size, META), :].astype(jnp.float32).astype(jnp.int32)
        meta_ref[pl.ds(8 * k, 8), :] = meta[:8]
    copy = pltpu.make_async_copy(meta_ref, index_ref, sem)
    copy.start()
    copy.wait()


def add_unit(k, slots, size, unit_ref, panel_ref, acc_ref, index_ref):
    for q, step in enumerate(slots[k]):
        row = index_ref[8 * k, q]
        col = index_ref[8 * k, len(slots[k]) + q]
        product = jnp.dot(
            unit_ref[pl.ds(q * size, size), :],
            panel_ref[step, pl.ds(pl.multiple_of(col * size, size), size), :],
            preferred_element_type=jnp.float32,
        )
        at = pl.ds(pl.multiple_of(row * size, size), size)
        acc_ref[at, :] = acc_ref[at, :] + product


def fold_kernel(*refs, slots, size):
    n = len(slots)
    unit_refs, (panel_ref, _, acc_ref, meta_ref, index_ref, sem) = refs[:n], refs[n:]
    read_index(slots, size, unit_refs, meta_ref, index_ref, sem)
    for k, unit_ref in enumerate(unit_refs):
        add_unit(k, slots, size, unit_ref, panel_ref, acc_ref, index_ref)


def last_kernel(*refs, slots, size):
    n = len(slots)
    unit_refs, (panel_ref, _, acc_ref, out_ref, meta_ref, index_ref, sem, out_sem) = refs[:n], refs[n:]
    read_index(slots, size, unit_refs, meta_ref, index_ref, sem)
    touched = [jnp.int32(0)]
    for k in reversed(range(n)):
        mask = touched[0]
        for q in range(len(slots[k])):
            row = index_ref[8 * k, q]
            mask = mask | jnp.where(row < RB_DEV, lax.shift_left(jnp.int32(1), row), 0)
        touched.insert(0, mask)

    def write(ready):
        for row in range(RB_DEV):
            at = pl.ds(row * size, size)

            @pl.when((lax.shift_right_logical(ready, jnp.int32(row)) & 1) == 1)
            def _():
                pltpu.make_async_copy(acc_ref.at[at], out_ref.at[at], out_sem).start()

    write(~touched[0])
    for k, unit_ref in enumerate(unit_refs):
        add_unit(k, slots, size, unit_ref, panel_ref, acc_ref, index_ref)
        write(touched[k] & ~touched[k + 1])
    pltpu.make_async_copy(acc_ref.at[pl.ds(0, out_ref.shape[0])], out_ref, out_sem).wait()


def fold(units, slots, panels, acc, last):
    n = len(units)
    size = units[0].shape[1]
    scen = panels.shape[2]
    vmem = pl.BlockSpec(memory_space=pltpu.VMEM)
    out_shape = [pltpu.VMEM(acc.shape, jnp.float32)]
    out_specs = [vmem]
    scratch = [pltpu.VMEM((8 * n, 128), jnp.int32), pltpu.SMEM((8 * n, 128), jnp.int32), pltpu.SemaphoreType.DMA]
    if last:
        out_shape.append(jax.ShapeDtypeStruct((RB_DEV * size, scen), jnp.float32))
        out_specs.append(pl.BlockSpec(memory_space=pltpu.HBM))
        scratch.append(pltpu.SemaphoreType.DMA)
    tiles = sum(len(held) for held in slots)
    return pl.pallas_call(
        functools.partial(last_kernel if last else fold_kernel, slots=slots, size=size),
        out_shape=tuple(out_shape),
        in_specs=[vmem] * (n + 2),
        out_specs=tuple(out_specs),
        input_output_aliases={n + 1: 0},
        scratch_shapes=scratch,
        compiler_params=pltpu.CompilerParams(vmem_limit_bytes=8 << 20),
        cost_estimate=pl.CostEstimate(
            flops=2 * tiles * size * size * scen, bytes_accessed=2 * tiles * size * size, transcendentals=0
        ),
        name="last" if last else "fold",
    )(*units, panels, acc)[-1]


def per_device(tiles, block_rows, block_cols, live_counts, panels, n_row, n_col):
    steps, _, per_dev, size, _ = tiles.shape
    parts, plan = gather_plan(n_col, steps * per_dev)
    slots = [[slot // per_dev for slot in range(low, high)] for low, high in parts]
    ring = [(i, (i + 1) % n_row) for i in range(n_row)]
    pieces = [panels]
    for _ in range(n_row - 1):
        pieces.append(lax.ppermute(pieces[-1], "row", ring))
    held = {(p, 0): unit for p, unit in enumerate(pack(block_rows, block_cols, live_counts, tiles, parts))}
    seen = set(held)
    folded = set()
    whole, acc = whole_panels(pieces, size)
    for step in plan:
        if isinstance(step, list):
            acc = fold([held[name] for name in step], [slots[p] for p, _ in step], whole, acc, False)
            folded.update(step)
            continue
        p, key, direction = step
        source = (p, origin(n_col, key, direction))
        seen.add(source)
        if folded:
            names = [name for name in held if name in seen]
            *tied, acc = lax.optimization_barrier((*(held[name] for name in names), acc))
            held.update(zip(names, tied))
        held[p, key] = hop(n_row, n_col, direction, held[source])
    rest = [name for name in held if name not in folded]
    return fold([held[name] for name in rest], [slots[p] for p, _ in rest], whole, acc, True)


def solution(mesh):
    placed = (
        P(None, "row", "col", None, None),
        P(None, "row", "col"),
        P(None, "row", "col"),
        P(None, "row", "col"),
        P(None, "row", "col"),
    )
    body = functools.partial(per_device, n_row=mesh.shape["row"], n_col=mesh.shape["col"])
    return jax.shard_map(body, mesh=mesh, in_specs=placed, out_specs=P("row", "col"), check_vma=False)
```

```python
import functools

import jax
import jax.numpy as jnp
from jax import lax
from jax.experimental import pallas as pl
from jax.experimental.pallas import tpu as pltpu
from jax.sharding import PartitionSpec as P

RB_DEV = 32
META = 16


PARTS = ((0, 12),)
PLAN = [
    (0, 2, 1),
    (0, 12, 3),
    (0, 1, 0),
    [(0, 0)],
    (0, 6, 2),
    (0, 13, 0),
    (0, 14, 1),
    [(0, 2), (0, 12)],
    (0, 5, 2),
    [(0, 1)],
    (0, 3, 0),
    (0, 4, 1),
    (0, 10, 2),
    [(0, 6), (0, 13)],
    (0, 7, 0),
    [(0, 14)],
    (0, 15, 1),
    [(0, 5)],
    (0, 9, 2),
    [(0, 3)],
    (0, 11, 0),
    (0, 8, 1),
    [(0, 10), (0, 4)],
    [(0, 7)],
    [(0, 15)],
]


def ring_of(n_col):
    return (0, 1, 3, 2) if n_col == 16 else tuple(range(n_col // 4))


def moved(n_col, index, direction):
    if direction < 2:
        return index ^ (1 + direction)
    ring = ring_of(n_col)
    at = ring.index(index // 4) + (1 if direction == 2 else -1)
    return ring[at % len(ring)] * 4 + index % 4


def hop(n_row, n_col, direction, unit):
    pairs = []
    for row in range(n_row):
        way = direction ^ 1 if row % 2 and direction < 2 else direction
        pairs += [(row * n_col + i, row * n_col + moved(n_col, i, way)) for i in range(n_col)]
    return lax.ppermute(unit, ("row", "col"), pairs)


def origin(n_col, key, direction):
    return (key ^ 1, key ^ 2, (key - 4) % n_col, (key + 4) % n_col)[direction]


def gather_plan(n_col, n_slots):
    if n_col == 16 and n_slots == PARTS[-1][1]:
        return PARTS, PLAN
    steps = []
    held = [0]
    ready = [(0, 0)]
    while len(held) < n_col:
        taken = []
        for direction in range(3):
            for key in range(1, n_col):
                if key not in held and key not in taken and origin(n_col, key, direction) in held:
                    steps.append((0, key, direction))
                    taken.append(key)
                    break
        steps.append(ready)
        held += taken
        ready = [(0, key) for key in taken]
    return ((0, n_slots),), steps


def pack_kernel(rows_hbm, cols_hbm, counts_hbm, tiles_ref, *refs, parts, size):
    unit_refs, (rows_ref, cols_ref, counts_ref, sem) = refs[: len(parts)], refs[len(parts) :]
    per_dev = rows_ref.shape[2]
    copies = [
        pltpu.make_async_copy(rows_hbm, rows_ref, sem.at[0]),
        pltpu.make_async_copy(cols_hbm, cols_ref, sem.at[1]),
        pltpu.make_async_copy(counts_hbm, counts_ref, sem.at[2]),
    ]
    for p, (low, high) in enumerate(parts):
        here = tiles_ref.at[pl.ds(low * size, (high - low) * size)]
        copies.append(pltpu.make_async_copy(here, unit_refs[p].at[pl.ds(0, (high - low) * size)], sem.at[3 + p]))
    for copy in copies:
        copy.start()
    for copy in copies[:3]:
        copy.wait()
    lane = lax.broadcasted_iota(jnp.int32, (META, 128), 1)
    for p, (low, high) in enumerate(parts):
        meta = jnp.zeros((META, 128), jnp.int32)
        for slot in range(low, high):
            step, q = slot // per_dev, slot % per_dev
            row = jnp.where(q < counts_ref[step], rows_ref[step, 0, q], RB_DEV)
            meta = jnp.where(lane == slot - low, row, meta)
            meta = jnp.where(lane == high - 2 * low + slot, cols_ref[step, 0, q], meta)
        unit_refs[p][pl.ds((high - low) * size, META), :] = meta.astype(jnp.float32).astype(jnp.bfloat16)
    for copy in copies[3:]:
        copy.wait()


def pack(rows, cols, counts, tiles, parts):
    steps, _, per_dev, size, _ = tiles.shape
    args = rows, cols, counts.reshape(steps), tiles.reshape(steps * per_dev * size, size)
    return pl.pallas_call(
        functools.partial(pack_kernel, parts=parts, size=size),
        out_shape=tuple(jax.ShapeDtypeStruct(((high - low) * size + META, size), jnp.bfloat16) for low, high in parts),
        in_specs=[pl.BlockSpec(memory_space=pltpu.HBM)] * 4,
        out_specs=(pl.BlockSpec(memory_space=pltpu.VMEM),) * len(parts),
        scratch_shapes=[
            pltpu.SMEM(rows.shape, jnp.int32),
            pltpu.SMEM(cols.shape, jnp.int32),
            pltpu.SMEM((steps,), jnp.int32),
            pltpu.SemaphoreType.DMA((3 + len(parts),)),
        ],
        compiler_params=pltpu.CompilerParams(vmem_limit_bytes=2 << 20),
        name="pack",
    )(*(pltpu.with_memory_space_constraint(x, pltpu.HBM) for x in args))


def panel_kernel(*refs, n_row):
    pieces, whole_ref, acc_ref, sem = refs[:n_row], refs[n_row], refs[n_row + 1], refs[n_row + 2]
    steps, depth, _ = pieces[0].shape
    me = lax.axis_index("row")
    copies = []
    for back_by, piece in enumerate(pieces):
        owner = lax.rem(me - back_by + n_row, n_row)
        for step in range(steps):
            copies.append(
                pltpu.make_async_copy(
                    piece.at[step],
                    whole_ref.at[step, pl.ds(owner * depth, depth)],
                    sem.at[back_by * steps + step],
                )
            )
    for copy in copies:
        copy.start()
    acc_ref[...] = jnp.zeros_like(acc_ref)
    for copy in copies:
        copy.wait()


def whole_panels(pieces, size):
    n_row = len(pieces)
    steps, depth, scen = pieces[0].shape
    return pl.pallas_call(
        functools.partial(panel_kernel, n_row=n_row),
        out_shape=(
            pltpu.VMEM((steps, n_row * depth, scen), jnp.bfloat16),
            pltpu.VMEM(((RB_DEV + 1) * size, scen), jnp.float32),
        ),
        in_specs=[pl.BlockSpec(memory_space=pltpu.HBM)] + [pl.BlockSpec(memory_space=pl.ANY)] * (n_row - 1),
        out_specs=(pl.BlockSpec(memory_space=pltpu.VMEM),) * 2,
        scratch_shapes=[pltpu.SemaphoreType.DMA((n_row * steps,))],
        compiler_params=pltpu.CompilerParams(vmem_limit_bytes=2 << 20),
        name="panels",
    )(pltpu.with_memory_space_constraint(pieces[0], pltpu.HBM), *pieces[1:])


def read_index(slots, size, unit_refs, meta_ref, index_ref, sem):
    for k, unit_ref in enumerate(unit_refs):
        meta = unit_ref[pl.ds(len(slots[k]) * size, META), :].astype(jnp.float32).astype(jnp.int32)
        meta_ref[pl.ds(8 * k, 8), :] = meta[:8]
    copy = pltpu.make_async_copy(meta_ref, index_ref, sem)
    copy.start()
    copy.wait()


def add_unit(k, slots, size, unit_ref, panel_ref, acc_ref, index_ref):
    for q, step in enumerate(slots[k]):
        row = index_ref[8 * k, q]
        col = index_ref[8 * k, len(slots[k]) + q]
        product = jnp.dot(
            unit_ref[pl.ds(q * size, size), :],
            panel_ref[step, pl.ds(pl.multiple_of(col * size, size), size), :],
            preferred_element_type=jnp.float32,
        )
        at = pl.ds(pl.multiple_of(row * size, size), size)
        acc_ref[at, :] = acc_ref[at, :] + product


def fold_kernel(*refs, slots, size):
    n = len(slots)
    unit_refs, (panel_ref, _, acc_ref, meta_ref, index_ref, sem) = refs[:n], refs[n:]
    read_index(slots, size, unit_refs, meta_ref, index_ref, sem)
    for k, unit_ref in enumerate(unit_refs):
        add_unit(k, slots, size, unit_ref, panel_ref, acc_ref, index_ref)


def last_kernel(*refs, slots, size):
    n = len(slots)
    unit_refs, (panel_ref, _, acc_ref, out_ref, meta_ref, index_ref, sem, out_sem) = refs[:n], refs[n:]
    read_index(slots, size, unit_refs, meta_ref, index_ref, sem)
    touched = [jnp.int32(0)]
    for k in reversed(range(n)):
        mask = touched[0]
        for q in range(len(slots[k])):
            row = index_ref[8 * k, q]
            mask = mask | jnp.where(row < RB_DEV, lax.shift_left(jnp.int32(1), row), 0)
        touched.insert(0, mask)

    def write(ready):
        for row in range(RB_DEV):
            at = pl.ds(row * size, size)

            @pl.when((lax.shift_right_logical(ready, jnp.int32(row)) & 1) == 1)
            def _():
                pltpu.make_async_copy(acc_ref.at[at], out_ref.at[at], out_sem).start()

    write(~touched[0])
    for k, unit_ref in enumerate(unit_refs):
        add_unit(k, slots, size, unit_ref, panel_ref, acc_ref, index_ref)
        write(touched[k] & ~touched[k + 1])
    pltpu.make_async_copy(acc_ref.at[pl.ds(0, out_ref.shape[0])], out_ref, out_sem).wait()


def fold(units, slots, panels, acc, last):
    n = len(units)
    size = units[0].shape[1]
    scen = panels.shape[2]
    vmem = pl.BlockSpec(memory_space=pltpu.VMEM)
    out_shape = [pltpu.VMEM(acc.shape, jnp.float32)]
    out_specs = [vmem]
    scratch = [pltpu.VMEM((8 * n, 128), jnp.int32), pltpu.SMEM((8 * n, 128), jnp.int32), pltpu.SemaphoreType.DMA]
    if last:
        out_shape.append(jax.ShapeDtypeStruct((RB_DEV * size, scen), jnp.float32))
        out_specs.append(pl.BlockSpec(memory_space=pltpu.HBM))
        scratch.append(pltpu.SemaphoreType.DMA)
    tiles = sum(len(held) for held in slots)
    return pl.pallas_call(
        functools.partial(last_kernel if last else fold_kernel, slots=slots, size=size),
        out_shape=tuple(out_shape),
        in_specs=[vmem] * (n + 2),
        out_specs=tuple(out_specs),
        input_output_aliases={n + 1: 0},
        scratch_shapes=scratch,
        compiler_params=pltpu.CompilerParams(vmem_limit_bytes=8 << 20),
        cost_estimate=pl.CostEstimate(
            flops=2 * tiles * size * size * scen, bytes_accessed=2 * tiles * size * size, transcendentals=0
        ),
        name="last" if last else "fold",
    )(*units, panels, acc)[-1]


def per_device(tiles, block_rows, block_cols, live_counts, panels, n_row, n_col):
    steps, _, per_dev, size, _ = tiles.shape
    parts, plan = gather_plan(n_col, steps * per_dev)
    slots = [[slot // per_dev for slot in range(low, high)] for low, high in parts]
    ring = [(i, (i + 1) % n_row) for i in range(n_row)]
    pieces = [panels]
    for _ in range(n_row - 1):
        pieces.append(lax.ppermute(pieces[-1], "row", ring))
    held = {(p, 0): unit for p, unit in enumerate(pack(block_rows, block_cols, live_counts, tiles, parts))}
    seen = set(held)
    folded = set()
    whole, acc = whole_panels(pieces, size)
    for step in plan:
        if isinstance(step, list):
            acc = fold([held[name] for name in step], [slots[p] for p, _ in step], whole, acc, False)
            folded.update(step)
            continue
        p, key, direction = step
        source = (p, origin(n_col, key, direction))
        seen.add(source)
        if folded:
            names = [name for name in held if name in seen]
            *tied, acc = lax.optimization_barrier((*(held[name] for name in names), acc))
            held.update(zip(names, tied))
        held[p, key] = hop(n_row, n_col, direction, held[source])
    rest = [name for name in held if name not in folded]
    return fold([held[name] for name in rest], [slots[p] for p, _ in rest], whole, acc, True)


def solution(mesh):
    placed = (
        P(None, "row", "col", None, None),
        P(None, "row", "col"),
        P(None, "row", "col"),
        P(None, "row", "col"),
        P(None, "row", "col"),
    )
    body = functools.partial(per_device, n_row=mesh.shape["row"], n_col=mesh.shape["col"])
    return jax.shard_map(body, mesh=mesh, in_specs=placed, out_specs=P("row", "col"), check_vma=False)
```
